128 devices in a mesh: row: 8 (over z_hi, y), col: 16 (over x, z_lo, core).
Axes of the slice: x: 4, y: 4, z: 4 (z_hi: 2, z_lo: 2; z = z_hi * 2 + z_lo), core: 2. Of those that a mesh axis runs over, the one named last changes fastest.
Arguments:
- features: bfloat16 [16, 8192, 128], P('col', 'row'), may hold values from 0.099609375 to 3
- relu_mask: int32 [16, 8192, 128], P('col', 'row'), may hold values 0 or 1
- tiles: bfloat16 [8, 16, 184, 256, 256], P('row', 'col'), may hold values from -0.25 to 0.25
- tile_rows: int32 [8, 16, 184], P('row', 'col'), may hold values from 0 to 63, as said below
- tile_cols: int32 [8, 16, 184], P('row', 'col'), may hold values from 0 to 31
- tile_count: int32 [8, 16], P('row', 'col'), may hold values from 23 to 184, as said below
- weight: bfloat16 [128, 128], replicated, may hold values from -0.5 to 0.5
- cotangent: bfloat16 [8, 16384, 128], P('row', 'col'), may hold values from -6 to 6
Outputs:
- out_pre: bfloat16 [8, 16384, 128], P('row', 'col')
- weight_grad: float32 [128, 128], replicated
- input_grad: bfloat16 [16, 8192, 128], P('col', 'row')
The draws below stay inside these ranges and needn't reach their ends.
Inputs may be any that keep to these rules, and one draw needn't show every extreme that they name: `tile_rows`: within one panel pair the live and dead slots name distinct (block row, block column) pairs. `tile_count`: counts differ widely between panel pairs.
All inputs are finite; a program needn't handle non-finite values. No bound on the sum of `relu_mask` on one device may be relied on, other than what follows from the above.
Results may differ from the reference program's by a relative error of at most 0.022.
Values may be sent and summed in bfloat16 or wider, within the bound.
A program may use at most 192 MiB of HBM per device.

```python
import math
import jax
import jax.numpy as jnp
from jax import lax

F = 128
TILE = 256
NODES_DEV = 1024
CAP = 184
ROW_PANEL = 16384
COL_PANEL = 8192
N_ROW = 8
N_COL = 16
DEVICES = 128


def tile_layout(key):
    base_key = jax.random.fold_in(key, 11)
    key_perm, key_level, key_full = jax.random.split(base_key, 3)
    row_blocks = NODES_DEV * N_COL // TILE
    col_blocks = NODES_DEV * N_ROW // TILE
    device_keys = jax.random.split(key_perm, N_ROW * N_COL)
    picks = jax.vmap(lambda one_key: jax.random.permutation(one_key, row_blocks * col_blocks)[:CAP])(device_keys)
    picks = picks.reshape(N_ROW, N_COL, CAP).astype(jnp.int32)
    levels = jax.random.randint(key_level, (N_ROW, N_COL), 0, 4).astype(jnp.int32)
    counts = jnp.int32(CAP) // jnp.left_shift(jnp.int32(1), levels)
    busiest = jax.random.randint(key_full, (), 0, N_ROW * N_COL).astype(jnp.int32)
    flat_ids = jnp.arange(N_ROW * N_COL, dtype=jnp.int32).reshape(N_ROW, N_COL)
    counts = jnp.where(flat_ids == busiest, jnp.int32(CAP), counts).astype(jnp.int32)
    return (picks // col_blocks, picks % col_blocks, counts)


def draw_tile_rows(key, part):
    return tile_layout(key)[0]


def draw_tile_cols(key, part):
    return tile_layout(key)[1]


def draw_tile_count(key, part):
    return tile_layout(key)[2]


def place_ends(result, key, low, largest):
    spot = [jax.random.randint(jax.random.fold_in(key, axis), (), 0, length) for axis, length in enumerate(result.shape)]
    main_axis = result.shape.index(max(result.shape))
    neighbour = spot[:main_axis] + [(spot[main_axis] + 1) % result.shape[main_axis]] + spot[main_axis + 1:]
    return result.at[tuple(spot)].set(low).at[tuple(neighbour)].set(largest)


def level_of(stream_key, shape, shards, low, largest):
    loudness = 1.0
    for position, shards_of in shards:
        heights = jax.random.uniform(jax.random.fold_in(jax.random.fold_in(stream_key, 6), position), (shards_of,), jnp.float32, low / len(shards), largest / len(shards))
        loudness = loudness * jnp.repeat(jnp.exp(heights), shape[position] // shards_of).reshape((-1,) + (1,) * (len(shape) - 1 - position))
    return loudness


def normal_values(stream_key, dims, spread, reach, shards=(), kind=jnp.bfloat16):
    array = spread * jax.random.normal(stream_key, dims, jnp.float32)
    if shards:
        array = array * level_of(stream_key, dims, shards, -0.22, 0.18)
    return jnp.clip(array, -reach, reach).astype(kind)


def setup_inputs(seed: int = 0) -> dict:
    key_list = jax.random.split(jax.random.key(seed), 9)
    features = jnp.clip(jnp.exp(math.log(3.0) - 3.4051113 * jax.random.uniform(key_list[0], (N_COL, COL_PANEL, F), jnp.float32) ** level_of(key_list[0], (N_COL, COL_PANEL, F), ((0, 16), (1, 8)), -0.2, 0.2)), 0.099609375, 3.0).astype(jnp.bfloat16)
    relu_mask = place_ends((jax.random.randint(key_list[1], (N_COL, COL_PANEL, F), 0, 2) < 1).astype(jnp.int32), jax.random.fold_in(key_list[1], 1), 0, 1)
    tiles = normal_values(key_list[2], (N_ROW, N_COL, CAP, TILE, TILE), ((CAP * TILE * TILE // (3 * NODES_DEV)) ** -0.5), 0.25, ((0, 8), (1, 16)))
    tile_rows = draw_tile_rows(jax.random.fold_in(key_list[8], 71), 0)
    tile_cols = draw_tile_cols(jax.random.fold_in(key_list[8], 71), 0)
    tile_count = draw_tile_count(jax.random.fold_in(key_list[8], 71), 0)
    weight = normal_values(key_list[6], (F, F), F ** -0.5, 0.5)
    cotangent = normal_values(key_list[7], (N_ROW, ROW_PANEL, F), 1.0, 6.0, ((0, 8), (1, 16)))
    return {"features": features, "relu_mask": relu_mask, "tiles": tiles, "tile_rows": tile_rows, "tile_cols": tile_cols, "tile_count": tile_count, "weight": weight, "cotangent": cotangent}


def forward_part(tile_vals, row_ids, col_ids, live_count, feat_panel):
    blocks = feat_panel.reshape(-1, TILE, F)[col_ids].astype(jnp.float32)
    products = jnp.einsum('sij,sjf->sif', tile_vals.astype(jnp.float32), blocks)
    live_slots = jnp.arange(CAP, dtype=jnp.int32) < live_count
    products = jnp.where(live_slots[:, None, None], products, 0.0)
    total = jax.ops.segment_sum(products, row_ids, num_segments=NODES_DEV * N_COL // TILE)
    return total.reshape(-1, F)

def backward_part(tile_vals, row_ids, col_ids, live_count, grad_rows):
    blocks = grad_rows.reshape(-1, TILE, F)[row_ids].astype(jnp.float32)
    products = jnp.einsum('sij,sif->sjf', tile_vals.astype(jnp.float32), blocks)
    live_slots = jnp.arange(CAP, dtype=jnp.int32) < live_count
    products = jnp.where(live_slots[:, None, None], products, 0.0)
    total = jax.ops.segment_sum(products, col_ids, num_segments=NODES_DEV * N_ROW // TILE)
    return total.reshape(-1, F)

def reference(features, relu_mask, tiles, tile_rows, tile_cols, tile_count, weight, cotangent):
    hidden = features * relu_mask.astype(jnp.bfloat16)

    def row_panel(row_index):

        def panel_step(running, inputs):
            tile_vals, row_ids, col_ids, live_count, feat_panel = inputs
            partial_value = forward_part(tile_vals, row_ids, col_ids, live_count, feat_panel)
            rounded = lax.optimization_barrier(partial_value.astype(jnp.bfloat16))
            return (running + rounded.astype(jnp.float32), None)
        running, unused = lax.scan(panel_step, jnp.zeros((NODES_DEV * N_COL, F), jnp.float32), (tiles[row_index], tile_rows[row_index], tile_cols[row_index], tile_count[row_index], hidden))
        return running.astype(jnp.bfloat16)
    aggregate = lax.map(row_panel, jnp.arange(N_ROW, dtype=jnp.int32))
    flat_agg = aggregate.reshape(-1, F)
    flat_cot = cotangent.reshape(-1, F)
    out_pre = jnp.dot(flat_agg, weight, preferred_element_type=jnp.float32).astype(jnp.bfloat16)
    out_pre = out_pre.reshape(N_ROW, NODES_DEV * N_COL, F)
    grad_scale = 1.0 / jnp.sqrt(jnp.float32(NODES_DEV * DEVICES))
    weight_grad = jnp.dot(flat_agg.T, flat_cot, preferred_element_type=jnp.float32) * grad_scale
    grad_agg = jnp.dot(flat_cot, weight.T, preferred_element_type=jnp.float32).astype(jnp.bfloat16)
    grad_agg = grad_agg.reshape(N_ROW, NODES_DEV * N_COL, F)

    def col_panel(col_index):

        def panel_step(running, inputs):
            tile_vals, row_ids, col_ids, live_count, grad_rows = inputs
            partial_value = backward_part(tile_vals, row_ids, col_ids, live_count, grad_rows)
            rounded = lax.optimization_barrier(partial_value.astype(jnp.bfloat16))
            return (running + rounded.astype(jnp.float32), None)
        running, unused = lax.scan(panel_step, jnp.zeros((NODES_DEV * N_ROW, F), jnp.float32), (tiles[:, col_index], tile_rows[:, col_index], tile_cols[:, col_index], tile_count[:, col_index], grad_agg))
        return running
    back_terms = lax.map(col_panel, jnp.arange(N_COL, dtype=jnp.int32))
    input_grad = (back_terms * relu_mask.astype(jnp.float32)).astype(jnp.bfloat16)
    return (out_pre, weight_grad, input_grad)
```

```python
import functools

import jax
import jax.numpy as jnp
from jax import lax
from jax.experimental import pallas as pl
from jax.experimental.pallas import tpu as pltpu
from jax.sharding import PartitionSpec as P

MESH = pl.DeviceIdType.MESH
F32 = jnp.float32
BF16 = jnp.bfloat16
UNROLL = 4
N_COPIES = 96


def plan(tile_rows, tile_cols, tile_count, row_blocks, col_blocks):
    slots = tile_rows.shape[0]
    ids = jnp.arange(slots, dtype=jnp.int32)
    dead = ids >= tile_count

    def one(target, source, targets, sources):
        key = target * sources + source + jnp.where(dead, targets * sources, 0)
        rank = jnp.sum((key[None, :] < key[:, None]).astype(jnp.int32), axis=1)
        hit = rank[:, None] == ids[None, :]

        def permute(values):
            return jnp.sum(jnp.where(hit, values[:, None], 0), axis=0)

        goal = jnp.where(dead, targets, target)
        same = (goal[:, None] == goal[None, :]) & (rank[None, :] < rank[:, None])
        head = 1 - jnp.max(same.astype(jnp.int32), axis=1)
        blocks = jnp.arange(targets, dtype=jnp.int32)
        upto = jnp.sum((goal[None, :] <= blocks[:, None]).astype(jnp.int32), axis=1)
        count = jnp.sum((goal[None, :] == blocks[:, None]).astype(jnp.int32), axis=1)
        last = jnp.maximum(upto - 1, 0)
        return [permute(ids), permute(source), permute(head), last, jnp.minimum(count, 1)]

    parts = one(tile_rows, tile_cols, row_blocks, col_blocks)
    parts += one(tile_cols, tile_rows, col_blocks, row_blocks)
    return jnp.concatenate(parts)


def kernel(
    slots, row_blocks, col_blocks, per, scale,
    tab, feat_hbm, mask_hbm, tiles_hbm, w_hbm, cot_hbm,
    out_ref, wg_ref, ig_ref,
    feat_v, mask_v, w_v, cot_v, tiles_v,
    hid, grd, prods, fpart, bpart, sib, xsum,
    ra, rb, fr, fl, zs, zb,
    acc_f, acc_b, agg, tb, ac, ax, ay, az, ws,
    send_sem, recv_sem, local_sem,
):
    r = lax.axis_index("row")
    c = lax.axis_index("col")
    zh, y = r // 4, lax.rem(r, 4)
    x, zl, core = c // 4, lax.rem(c // 2, 2), lax.rem(c, 2)

    def col_of(xx, zz, kk):
        return xx * 4 + zz * 2 + kk

    def at_x(step):
        return lax.rem(x + step, 4)

    def at_y(step):
        return lax.rem(y + step, 4)

    def x_dev(step):
        return {"row": r, "col": col_of(at_x(step), zl, core)}

    def y_dev(step):
        return {"row": zh * 4 + at_y(step), "col": c}

    sib_dev = {"row": r, "col": col_of(x, zl, 1 - core)}
    zl_dev = {"row": r, "col": col_of(x, 1 - zl, core)}
    zh_dev = {"row": (1 - zh) * 4 + y, "col": c}
    zz_dev = {"row": (1 - zh) * 4 + y, "col": col_of(x, 1 - zl, core)}
    right, left, up, down = x_dev(1), x_dev(3), y_dev(1), y_dev(3)
    peers = [sib_dev, right, left, x_dev(2), up, down, y_dev(2), zl_dev, zh_dev, zz_dev]

    loads = [(feat_hbm, feat_v), (mask_hbm, mask_v), (w_hbm, w_v), (cot_hbm, cot_v), (tiles_hbm, tiles_v)]
    loads = [pltpu.make_async_copy(s, d, local_sem.at[i]) for i, (s, d) in enumerate(loads)]
    for load in loads:
        load.start()

    barrier = pltpu.get_barrier_semaphore()
    for peer in peers:
        pl.semaphore_signal(barrier, inc=1, device_id=peer, device_id_type=MESH)

    made = []

    def send(src, dst, dev):
        i = len(made)
        copy = pltpu.make_async_remote_copy(
            src_ref=src, dst_ref=dst, send_sem=send_sem.at[i], recv_sem=recv_sem.at[i],
            device_id=dev, device_id_type=MESH,
        )
        copy.start()
        made.append(copy)
        return copy

    half = per // 2

    def col_shard(xx, zz, kk, first=0, size=per):
        return grd.at[pl.ds(col_of(xx, zz, kk) * per + first, size)]

    def row_shard(zz, yy, first=0, size=per):
        return hid.at[pl.ds((zz * 4 + yy) * per + first, size)]

    def share(ref, dev):
        return send(ref, ref, dev)

    loads[2].wait()
    loads[3].wait()
    for j in range(per):
        block = lax.dot_general(
            w_v[...], cot_v[j * 256 : (j + 1) * 256], (((1,), (1,)), ((), ())), preferred_element_type=F32
        )
        grd[c * per + j] = block.astype(BF16)
    loads[0].wait()
    loads[1].wait()
    for j in range(per):
        rows = slice(j * 256, (j + 1) * 256)
        hid[r * per + j] = feat_v[rows] * mask_v[rows].astype(F32).astype(BF16)

    pl.semaphore_wait(barrier, len(peers))

    c_r = share(col_shard(x, zl, core), right)
    c_l = share(col_shard(x, zl, core), left)
    r_u = share(row_shard(zh, y), up)
    r_d = share(row_shard(zh, y), down)
    r_z = share(row_shard(zh, y), zh_dev)
    c_z = share(col_shard(x, zl, core), zl_dev)
    c_s = [share(col_shard(x, zl, core), sib_dev)]

    c_z.wait_recv()
    cz_r = share(col_shard(x, 1 - zl, core), right)
    cz_l = share(col_shard(x, 1 - zl, core), left)
    c_s.append(share(col_shard(x, 1 - zl, core), sib_dev))
    r_z.wait_recv()
    rz_u = share(row_shard(1 - zh, y), up)
    rz_d = share(row_shard(1 - zh, y), down)

    def relay_x(from_left, from_right, zz):
        from_left.wait_recv()
        a = share(col_shard(at_x(3), zz, core, 0, half), right)
        c_s.append(share(col_shard(at_x(3), zz, core), sib_dev))
        from_right.wait_recv()
        b = share(col_shard(at_x(1), zz, core, half, half), left)
        c_s.append(share(col_shard(at_x(1), zz, core), sib_dev))
        return a, b

    def relay_y(from_down, from_up, zz):
        from_down.wait_recv()
        a = share(row_shard(zz, at_y(3), 0, half), up)
        from_up.wait_recv()
        b = share(row_shard(zz, at_y(1), half, half), down)
        return a, b

    ya, yb = relay_y(r_u, r_d, zh)
    xa, xb = relay_x(c_r, c_l, zl)
    yza, yzb = relay_y(rz_u, rz_d, 1 - zh)
    xza, xzb = relay_x(cz_r, cz_l, 1 - zl)
    for copy in (ya, yb, yza, yzb):
        copy.wait_recv()
    loads[4].wait()

    o_f = 0
    o_b = 3 * slots + 2 * row_blocks

    def fwd_range(lo, hi):
        @pl.loop(lo, hi)
        def _(g):
            acc = acc_f[...]
            for u in range(UNROLL):
                p = g * UNROLL + u
                prod = jnp.dot(
                    tiles_v[tab[o_f + p]], hid[tab[o_f + slots + p]], preferred_element_type=F32
                )
                acc = jnp.where(tab[o_f + 2 * slots + p] == 1, 0.0, acc) + prod
                prods[p] = acc.astype(BF16)
            acc_f[...] = acc

    def bwd_range(lo, hi):
        @pl.loop(lo, hi)
        def _(g):
            acc = acc_b[...]
            for u in range(UNROLL):
                p = g * UNROLL + u
                prod = jnp.dot(
                    grd[tab[o_b + slots + p]], tiles_v[tab[o_b + p]], preferred_element_type=F32
                )
                acc = jnp.where(tab[o_b + 2 * slots + p] == 1, 0.0, acc) + prod
                prods[p, 0:128, :] = acc[:, 0:128].astype(BF16)
                prods[p, 128:256, :] = acc[:, 128:256].astype(BF16)
            acc_b[...] = acc

    groups = slots // UNROLL
    acc_f[...] = jnp.zeros_like(acc_f)
    acc_b[...] = jnp.zeros_like(acc_b)

    fwd_range(0, groups // 2)
    for copy, zz, sx, first in ((xa, zl, 3, 0), (xb, zl, 1, half)):
        copy.wait_recv()
        c_s.append(share(col_shard(at_x(2), zz, core, first, half), sib_dev))
    fwd_range(groups // 2, groups)
    for copy, zz, first in ((xza, 1 - zl, 0), (xzb, 1 - zl, half)):
        copy.wait_recv()
        c_s.append(share(col_shard(at_x(2), zz, core, first, half), sib_dev))

    def take(dst, block, offset, targets):
        i = offset + 3 * slots + block
        value = prods[tab[i]]
        dst[block] = jnp.where(tab[i + targets] == 1, value, jnp.zeros_like(value))

    zs_of = (1 - zl, zl)

    def fill(kk):
        @pl.loop(0, row_blocks // 2)
        def _(m):
            take(fpart, (m // per) * 2 * per + kk * per + lax.rem(m, per), o_f, row_blocks)

    fill(1 - core)
    sibs = {}
    for dz in range(2):
        for dx in (2, 1, 3, 0):
            src = fpart.at[pl.ds(col_of(at_x(dx), zs_of[dz], 1 - core) * per, per)]
            sibs[dz, dx] = send(src, sib.at[dz, dx], sib_dev)
    fill(core)

    def with_sibling(dz, dx):
        sibs[dz, dx].wait_recv()
        base = col_of(at_x(dx), zs_of[dz], core) * per

        @pl.loop(0, per)
        def _(j):
            xsum[dz, dx, j] = (fpart[base + j].astype(F32) + sib[dz, dx, j].astype(F32)).astype(BF16)

    def add_into(dst, first, other):
        @pl.loop(0, half)
        def _(j):
            dst[first + j] = (dst[first + j].astype(F32) + other[j].astype(F32)).astype(BF16)

    def ring_sum(k, part, prepare, ahead, behind, z_dev, finish):
        a, b = (0, half), (half, half)

        def piece(dz, d, ab):
            return part(dz, d).at[pl.ds(ab[0], ab[1])]

        first, second = {}, {}

        def far(dz):
            prepare(dz, 2)
            first[dz] = (
                send(piece(dz, 2, a), ra.at[k, dz], ahead),
                send(piece(dz, 2, b), rb.at[k, dz], behind),
            )

        def near(dz):
            prepare(dz, 1)
            prepare(dz, 3)
            second[dz] = [
                send(piece(dz, 1, b), fr.at[k, dz, pl.ds(half, half)], ahead),
                send(piece(dz, 3, a), fl.at[k, dz, pl.ds(0, half)], behind),
            ]

        def relay(dz):
            first[dz][0].wait_recv()
            add_into(part(dz, 1), 0, ra.at[k, dz])
            second[dz].append(send(piece(dz, 1, a), fr.at[k, dz, pl.ds(0, half)], ahead))
            first[dz][1].wait_recv()
            add_into(part(dz, 3), half, rb.at[k, dz])
            second[dz].append(send(piece(dz, 3, b), fl.at[k, dz, pl.ds(half, half)], behind))

        def total(dz, j):
            return part(dz, 0)[j].astype(F32) + fr[k, dz, j].astype(F32) + fl[k, dz, j].astype(F32)

        far(0)
        near(0)
        far(1)
        yield
        relay(0)
        near(1)
        yield
        relay(1)
        prepare(0, 0)
        prepare(1, 0)
        yield
        for copy in second[0]:
            copy.wait_recv()

        @pl.loop(0, per)
        def _(j):
            zs[k, j] = total(0, j).astype(BF16)

        last = send(zs.at[k], zb.at[k], z_dev)
        yield
        for copy in second[1]:
            copy.wait_recv()
        last.wait_recv()
        for j in range(per):
            finish(j, total(1, j) + zb[k, j].astype(F32))

    def finish_f(j, value):
        agg[j * 256 : (j + 1) * 256] = value.astype(BF16)

    def finish_b(j, value):
        for h in range(2):
            rows = slice(j * 256 + h * 128, j * 256 + h * 128 + 128)
            ig_ref[rows] = (value[h * 128 : (h + 1) * 128].T * mask_v[rows].astype(F32)).astype(BF16)

    sum_f = ring_sum(0, lambda dz, d: xsum.at[dz, d], with_sibling, right, left, zl_dev, finish_f)

    zh_of = (1 - zh, zh)
    sum_b = ring_sum(
        1,
        lambda dz, d: bpart.at[pl.ds((zh_of[dz] * 4 + at_y(d)) * per, per)],
        lambda dz, d: None,
        up, down, zh_dev, finish_b,
    )

    for copy in c_s:
        copy.wait_recv()
    bounds = [groups * i // 4 for i in range(5)]
    bwd_range(bounds[0], bounds[1])
    next(sum_f)
    bwd_range(bounds[1], bounds[2])
    next(sum_f)
    bwd_range(bounds[2], bounds[3])
    next(sum_f)
    bwd_range(bounds[3], bounds[4])

    @pl.loop(0, col_blocks)
    def _(m):
        take(bpart, m, o_b, col_blocks)

    next(sum_b)
    next(sum_f)
    next(sum_b)
    next(sum_f, None)

    out_ref[...] = jnp.dot(agg[...], w_v[...], preferred_element_type=F32).astype(BF16)
    tb[...] = lax.dot_general(agg[...], cot_v[...], (((0,), (0,)), ((), ())), preferred_element_type=F32)
    rows = tb.shape[0] // 2
    to_sib = send(tb.at[pl.ds((1 - core) * rows, rows)], ac, sib_dev)
    next(sum_b)
    to_sib.wait_recv()
    ax[x] = tb[pl.ds(core * rows, rows)] + ac[...]
    ring = [send(ax.at[x], ax.at[x], x_dev(s)) for s in (1, 3, 2)]
    next(sum_b)
    for copy in ring:
        copy.wait_recv()
    ay[y] = (ax[0] + ax[1]) + (ax[2] + ax[3])
    ring = [send(ay.at[y], ay.at[y], y_dev(s)) for s in (1, 3, 2)]
    next(sum_b, None)
    for copy in ring:
        copy.wait_recv()
    z = zh * 2 + zl
    az[z] = (ay[0] + ay[1]) + (ay[2] + ay[3])
    ring = [send(az.at[z], az.at[z], dev) for dev in (zl_dev, zh_dev, zz_dev)]
    for copy in ring:
        copy.wait_recv()
    ws[core] = ((az[0] + az[1]) + (az[2] + az[3])) * scale
    last = share(ws.at[core], sib_dev)
    last.wait_recv()
    wg_ref[0:rows] = ws[0]
    wg_ref[rows : 2 * rows] = ws[1]

    for copy in made:
        copy.wait_send()


def body(features, relu_mask, tiles, tile_rows, tile_cols, tile_count, weight, cotangent):
    slots, tile = tiles.shape[2], tiles.shape[3]
    own, width = features.shape[1:]
    per = own // tile
    row_blocks, col_blocks = per * lax.axis_size("col"), per * lax.axis_size("row")
    half = per // 2
    scale = float((own * lax.axis_size("row") * lax.axis_size("col")) ** -0.5)
    table = plan(tile_rows[0, 0], tile_cols[0, 0], tile_count[0, 0], row_blocks, col_blocks)
    block = (tile, width)
    v = pltpu.VMEM
    anywhere = pl.BlockSpec(memory_space=pl.ANY)
    in_vmem = pl.BlockSpec(memory_space=pltpu.VMEM)
    out_pre, weight_grad, input_grad = pl.pallas_call(
        functools.partial(kernel, slots, row_blocks, col_blocks, per, scale),
        out_shape=(
            jax.ShapeDtypeStruct((own, width), BF16),
            jax.ShapeDtypeStruct((width, width), F32),
            jax.ShapeDtypeStruct((own, width), BF16),
        ),
        in_specs=[pl.BlockSpec(memory_space=pltpu.SMEM)] + [anywhere] * 5,
        out_specs=(in_vmem,) * 3,
        scratch_shapes=[
            v((own, width), BF16),
            v((own, width), jnp.int32),
            v((width, width), BF16),
            v((own, width), BF16),
            v((slots, tile, tile), BF16),
            v((col_blocks,) + block, BF16),
            v((row_blocks, width, tile), BF16),
            v((slots,) + block, BF16),
            v((row_blocks,) + block, BF16),
            v((col_blocks,) + block, BF16),
            v((2, 4, per) + block, BF16),
            v((2, 4, per) + block, BF16),
            v((2, 2, half) + block, BF16),
            v((2, 2, half) + block, BF16),
            v((2, 2, per) + block, BF16),
            v((2, 2, per) + block, BF16),
            v((2, per) + block, BF16),
            v((2, per) + block, BF16),
            v(block, F32),
            v((width, tile), F32),
            v((own, width), BF16),
            v((width, width), F32),
            v((width // 2, width), F32),
            v((4, width // 2, width), F32),
            v((4, width // 2, width), F32),
            v((4, width // 2, width), F32),
            v((2, width // 2, width), F32),
            pltpu.SemaphoreType.DMA((N_COPIES,)),
            pltpu.SemaphoreType.DMA((N_COPIES,)),
            pltpu.SemaphoreType.DMA((5,)),
        ],
        compiler_params=pltpu.CompilerParams(
            collective_id=0, has_side_effects=True, vmem_limit_bytes=67043328
        ),
        name="layer",
    )(table, features[0], relu_mask[0], tiles[0, 0], weight, cotangent[0])
    return out_pre[None], weight_grad, input_grad[None]


def solution(mesh):
    placed = (
        P("col", "row", None),
        P("col", "row", None),
        P("row", "col", None, None, None),
        P("row", "col", None),
        P("row", "col", None),
        P("row", "col"),
        P(),
        P("row", "col", None),
    )
    return jax.shard_map(
        body,
        mesh=mesh,
        in_specs=placed,
        out_specs=(P("row", "col", None), P(), P("col", "row", None)),
        check_vma=False,
    )
```

```python
import functools

import jax
import jax.numpy as jnp
from jax import lax
from jax.experimental import pallas as pl
from jax.experimental.pallas import tpu as pltpu
from jax.sharding import PartitionSpec as P

MESH = pl.DeviceIdType.MESH
F32 = jnp.float32
BF16 = jnp.bfloat16
UNROLL = 23
N_COPIES = 104
PAD = 256


def sorted_slots(rows, cols, count, row_blocks, col_blocks):
    n = rows.shape[1]
    across = lax.broadcasted_iota(jnp.int32, (n, n), 1)
    downward = lax.broadcasted_iota(jnp.int32, (n, n), 0)
    ids = across[0:1]
    down_ids = downward[:, 0:1]
    dead = ids >= count

    def column(row):
        return jnp.sum(jnp.where(across == downward, row, 0), axis=1, keepdims=True)

    def one(target, source, targets, sources):
        key = jnp.where(dead, targets * sources + ids, target * sources + source)
        goal = jnp.where(dead, targets, target)
        goal_c = column(goal)
        before = key < column(key)
        rank = jnp.sum(jnp.where(before, 1, 0), axis=1, keepdims=True)
        again = jnp.sum(jnp.where(before & (goal == goal_c), 1, 0), axis=1, keepdims=True)
        head = jnp.where(again == 0, 1, 0)
        packed = down_ids * 256 + column(source) * 2 + head
        order = jnp.sum(jnp.where(rank == across, packed, 0), axis=0, keepdims=True)
        upto = jnp.sum(jnp.where(goal_c <= across, 1, 0), axis=0, keepdims=True)
        some = jnp.sum(jnp.where(goal_c == across, 1, 0), axis=0, keepdims=True)
        return order, jnp.maximum(upto - 1, 0) * 2 + jnp.where(some > 0, 1, 0)

    order_f, last_f = one(rows, cols, row_blocks, col_blocks)
    order_b, last_b = one(cols, rows, col_blocks, row_blocks)
    return order_f, order_b, last_f, last_b


def kernel(
    slots, row_blocks, col_blocks, per, scale,
    feat_hbm, mask_hbm, w_hbm, cot_hbm, rows_hbm, cols_hbm, count_hbm, tiles_hbm,
    out_ref, wg_ref, ig_ref,
    feat_v, mask_v, w_v, cot_v, rows_v, cols_v, count_s, pair_v, tiles_v, tab_v, tab,
    hid, grd, prods, fpart, bpart, sib, xsum,
    ra, rb, fr, fl, zs, zb,
    acc_f, acc_b, agg, tb, ac, ax, ay, az, ws,
    send_sem, recv_sem, local_sem,
):
    r = lax.axis_index("row")
    c = lax.axis_index("col")
    zh, y = r // 4, lax.rem(r, 4)
    x, zl, core = c // 4, lax.rem(c // 2, 2), lax.rem(c, 2)

    def col_of(xx, zz, kk):
        return xx * 4 + zz * 2 + kk

    def at_x(step):
        return lax.rem(x + step, 4)

    def at_y(step):
        return lax.rem(y + step, 4)

    def x_dev(step):
        return {"row": r, "col": col_of(at_x(step), zl, core)}

    def y_dev(step):
        return {"row": zh * 4 + at_y(step), "col": c}

    sib_dev = {"row": r, "col": col_of(x, zl, 1 - core)}
    zl_dev = {"row": r, "col": col_of(x, 1 - zl, core)}
    zh_dev = {"row": (1 - zh) * 4 + y, "col": c}
    zz_dev = {"row": (1 - zh) * 4 + y, "col": col_of(x, 1 - zl, core)}
    right, left, up, down = x_dev(1), x_dev(3), y_dev(1), y_dev(3)
    peers = [sib_dev, right, left, x_dev(2), up, down, y_dev(2), zl_dev, zh_dev, zz_dev]

    barrier = pltpu.get_barrier_semaphore()
    for peer in peers:
        pl.semaphore_signal(barrier, inc=1, device_id=peer, device_id_type=MESH)

    loads = [
        (feat_hbm, feat_v), (mask_hbm, mask_v), (w_hbm, w_v), (cot_hbm, cot_v),
        (rows_hbm, rows_v), (cols_hbm, cols_v),
        (count_hbm, count_s), (tiles_hbm, tiles_v),
    ]
    loads = [pltpu.make_async_copy(src, dst, local_sem.at[i]) for i, (src, dst) in enumerate(loads)]
    for load in loads:
        load.start()

    made = []

    def send(src, dst, dev):
        i = len(made)
        copy = pltpu.make_async_remote_copy(
            src_ref=src, dst_ref=dst, send_sem=send_sem.at[i], recv_sem=recv_sem.at[i],
            device_id=dev, device_id_type=MESH,
        )
        copy.start()
        made.append(copy)
        return copy

    half = per // 2

    def col_shard(xx, zz, kk, first=0, size=per):
        return grd.at[pl.ds(col_of(xx, zz, kk) * per + first, size)]

    def row_shard(zz, yy, first=0, size=per):
        return hid.at[pl.ds((zz * 4 + yy) * per + first, size)]

    def share(ref, dev):
        return send(ref, ref, dev)

    first, second = (0, half), (half, half)

    loads[0].wait()
    loads[1].wait()
    for j in range(per):
        rows = slice(j * 256, (j + 1) * 256)
        hid[r * per + j] = feat_v[rows] * mask_v[rows].astype(F32).astype(BF16)

    pl.semaphore_wait(barrier, len(peers))

    def spread_y(zz):
        a = share(row_shard(zz, y, *first), up)
        b = share(row_shard(zz, y, *second), down)
        return a, b, [share(row_shard(zz, y, *second), up), share(row_shard(zz, y, *first), down)]

    def relay_y(a, b, zz):
        a.wait_recv()
        on = [share(row_shard(zz, at_y(3), *first), up)]
        b.wait_recv()
        on.append(share(row_shard(zz, at_y(1), *second), down))
        return on

    def spread_x(zz):
        a = share(col_shard(x, zz, core, *first), right)
        b = share(col_shard(x, zz, core, *second), left)
        rest = [share(col_shard(x, zz, core, *second), right), share(col_shard(x, zz, core, *first), left)]
        c_s.append(share(col_shard(x, zz, core), sib_dev))
        return a, b, rest

    def relay_x(a, b, zz):
        a.wait_recv()
        on = [share(col_shard(at_x(3), zz, core, *first), right)]
        b.wait_recv()
        on.append(share(col_shard(at_x(1), zz, core, *second), left))
        return on

    def cross_near(rest, zz):
        rest[0].wait_recv()
        c_s.append(share(col_shard(at_x(3), zz, core), sib_dev))
        rest[1].wait_recv()
        c_s.append(share(col_shard(at_x(1), zz, core), sib_dev))

    def cross_far(on, zz):
        for copy in on:
            copy.wait_recv()
        c_s.append(share(col_shard(at_x(2), zz, core), sib_dev))

    c_s = []
    ra_y, rb_y, r_rest = spread_y(zh)
    r_z = share(row_shard(zh, y), zh_dev)

    loads[2].wait()
    loads[3].wait()
    for j in range(per):
        block = lax.dot_general(
            w_v[...], cot_v[j * 256 : (j + 1) * 256], (((1,), (1,)), ((), ())), preferred_element_type=F32
        )
        grd[c * per + j] = block.astype(BF16)
    ca_x, cb_x, c_rest = spread_x(zl)

    for load in loads[4:7]:
        load.wait()
    pair_v[...] = jnp.zeros_like(pair_v)
    pair_v[0:1, 0:slots] = rows_v[...]
    pair_v[1:2, 0:slots] = cols_v[...]
    table = sorted_slots(pair_v[0:1], pair_v[1:2], count_s[0, 0], row_blocks, col_blocks)
    for i, line in enumerate(table):
        tab_v[i : i + 1] = line
    to_smem = pltpu.make_async_copy(tab_v, tab, local_sem.at[8])
    to_smem.start()

    r_on = relay_y(ra_y, rb_y, zh)
    c_on = relay_x(ca_x, cb_x, zl)
    r_z.wait_recv()
    za_y, zb_y, rz_rest = spread_y(1 - zh)
    c_z = share(col_shard(x, zl, core), zl_dev)
    cross_near(c_rest, zl)
    rz_on = relay_y(za_y, zb_y, 1 - zh)
    cross_far(c_on, zl)
    c_z.wait_recv()
    za_x, zb_x, cz_rest = spread_x(1 - zl)
    to_smem.wait()
    loads[7].wait()
    for copy in (*r_rest, *r_on, *rz_rest, *rz_on):
        copy.wait_recv()

    def fwd_range(lo, hi):
        @pl.loop(lo, hi)
        def _(g):
            acc = acc_f[...]
            for u in range(UNROLL):
                p = g * UNROLL + u
                word = tab[0, p]
                prod = jnp.dot(tiles_v[word >> 8], hid[(word >> 1) & 127], preferred_element_type=F32)
                acc = jnp.where((word & 1) == 1, 0.0, acc) + prod
                prods[p] = acc.astype(BF16)
            acc_f[...] = acc

    def bwd_range(lo, hi):
        @pl.loop(lo, hi)
        def _(g):
            acc = acc_b[...]
            for u in range(UNROLL):
                p = g * UNROLL + u
                word = tab[1, p]
                prod = jnp.dot(grd[(word >> 1) & 127], tiles_v[word >> 8], preferred_element_type=F32)
                acc = jnp.where((word & 1) == 1, 0.0, acc) + prod
                prods[p, 0:128, :] = acc[:, 0:128].astype(BF16)
                prods[p, 128:256, :] = acc[:, 128:256].astype(BF16)
            acc_b[...] = acc

    groups = slots // UNROLL
    acc_f[...] = jnp.zeros_like(acc_f)
    acc_b[...] = jnp.zeros_like(acc_b)

    fwd_range(0, groups // 4)
    cz_on = relay_x(za_x, zb_x, 1 - zl)
    cross_near(cz_rest, 1 - zl)
    fwd_range(groups // 4, groups)
    cross_far(cz_on, 1 - zl)

    def take(dst, line, base):
        for j in range(per):
            word = tab[line, base + j]
            value = prods[word >> 1]
            dst[base + j] = jnp.where((word & 1) == 1, value, jnp.zeros_like(value))

    zs_of = (1 - zl, zl)
    sibs = {}
    for dz in range(2):
        for dx in (2, 1, 3, 0):
            base = col_of(at_x(dx), zs_of[dz], 1 - core) * per
            take(fpart, 2, base)
            sibs[dz, dx] = send(fpart.at[pl.ds(base, per)], sib.at[dz, dx], sib_dev)

    @pl.loop(0, row_blocks // (2 * per))
    def _(m):
        take(fpart, 2, (2 * m + core) * per)

    def with_sibling(dz, dx):
        sibs[dz, dx].wait_recv()
        base = col_of(at_x(dx), zs_of[dz], core) * per
        for j in range(per):
            xsum[dz, dx, j] = (fpart[base + j].astype(F32) + sib[dz, dx, j].astype(F32)).astype(BF16)

    def add_into(dst, start, other):
        for j in range(half):
            dst[start + j] = (dst[start + j].astype(F32) + other[j].astype(F32)).astype(BF16)

    def ring_sum(k, part, prepare, ahead, behind, z_dev, finish):
        a, b = first, second

        def piece(dz, d, ab):
            return part(dz, d).at[pl.ds(ab[0], ab[1])]

        outer, inner = {}, {}

        def far(dz):
            prepare(dz, 2)
            outer[dz] = (
                send(piece(dz, 2, a), ra.at[k, dz], ahead),
                send(piece(dz, 2, b), rb.at[k, dz], behind),
            )

        def near(dz):
            prepare(dz, 1)
            prepare(dz, 3)
            inner[dz] = [
                send(piece(dz, 1, b), fr.at[k, dz, pl.ds(half, half)], ahead),
                send(piece(dz, 3, a), fl.at[k, dz, pl.ds(0, half)], behind),
            ]

        def relay(dz):
            outer[dz][0].wait_recv()
            add_into(part(dz, 1), 0, ra.at[k, dz])
            inner[dz].append(send(piece(dz, 1, a), fr.at[k, dz, pl.ds(0, half)], ahead))
            outer[dz][1].wait_recv()
            add_into(part(dz, 3), half, rb.at[k, dz])
            inner[dz].append(send(piece(dz, 3, b), fl.at[k, dz, pl.ds(half, half)], behind))

        def total(dz, j):
            return part(dz, 0)[j].astype(F32) + fr[k, dz, j].astype(F32) + fl[k, dz, j].astype(F32)

        far(0)
        near(0)
        yield
        relay(0)
        far(1)
        near(1)
        prepare(0, 0)
        yield
        for copy in inner[0]:
            copy.wait_recv()
        for j in range(per):
            zs[k, j] = total(0, j).astype(BF16)
        last = send(zs.at[k], zb.at[k], z_dev)
        prepare(1, 0)
        yield
        relay(1)
        yield
        for copy in inner[1]:
            copy.wait_recv()
        last.wait_recv()
        for j in range(per):
            finish(j, total(1, j) + zb[k, j].astype(F32))

    def finish_f(j, value):
        agg[j * 256 : (j + 1) * 256] = value.astype(BF16)

    def finish_b(j, value):
        for h in range(2):
            rows = slice(j * 256 + h * 128, j * 256 + h * 128 + 128)
            ig_ref[rows] = (value[h * 128 : (h + 1) * 128].T * mask_v[rows].astype(F32)).astype(BF16)

    sum_f = ring_sum(0, lambda dz, d: xsum.at[dz, d], with_sibling, right, left, zl_dev, finish_f)

    zh_of = (1 - zh, zh)
    sum_b = ring_sum(
        1,
        lambda dz, d: bpart.at[pl.ds((zh_of[dz] * 4 + at_y(d)) * per, per)],
        lambda dz, d: None,
        up, down, zh_dev, finish_b,
    )

    for copy in c_s:
        copy.wait_recv()
    bwd_range(0, groups // 4)
    next(sum_f)
    bwd_range(groups // 4, groups)

    @pl.loop(0, col_blocks // per)
    def _(m):
        take(bpart, 3, m * per)

    next(sum_b)
    next(sum_f)
    next(sum_b)
    next(sum_f)
    next(sum_f)
    next(sum_b)
    next(sum_b)
    next(sum_f, None)

    tb[...] = lax.dot_general(agg[...], cot_v[...], (((0,), (0,)), ((), ())), preferred_element_type=F32)
    rows = tb.shape[0] // 2
    to_sib = send(tb.at[pl.ds((1 - core) * rows, rows)], ac, sib_dev)
    out_ref[...] = jnp.dot(agg[...], w_v[...], preferred_element_type=F32).astype(BF16)
    to_sib.wait_recv()

    def ring_add(slots_ref, at, value, devices):
        slots_ref[at] = value
        copies = [send(slots_ref.at[at], slots_ref.at[at], dev) for dev in devices]
        for copy in copies:
            copy.wait_recv()
        return (slots_ref[0] + slots_ref[1]) + (slots_ref[2] + slots_ref[3])

    term = tb[pl.ds(core * rows, rows)] + ac[...]
    term = ring_add(ax, x, term, [x_dev(step) for step in (1, 3, 2)])
    term = ring_add(az, zh * 2 + zl, term, [zl_dev, zh_dev, zz_dev])
    term = ring_add(ay, y, term, [y_dev(step) for step in (1, 3, 2)])
    ws[core] = term * scale
    last = share(ws.at[core], sib_dev)
    next(sum_b, None)
    last.wait_recv()
    wg_ref[0:rows] = ws[0]
    wg_ref[rows : 2 * rows] = ws[1]

    for copy in made:
        copy.wait_send()


def body(features, relu_mask, tiles, tile_rows, tile_cols, tile_count, weight, cotangent):
    slots, tile = tiles.shape[2], tiles.shape[3]
    own, width = features.shape[1:]
    per = own // tile
    row_blocks, col_blocks = per * lax.axis_size("col"), per * lax.axis_size("row")
    half = per // 2
    scale = float((own * lax.axis_size("row") * lax.axis_size("col")) ** -0.5)
    block = (tile, width)
    v = pltpu.VMEM
    anywhere = pl.BlockSpec(memory_space=pl.ANY)
    in_vmem = pl.BlockSpec(memory_space=pltpu.VMEM)
    out_pre, weight_grad, input_grad = pl.pallas_call(
        functools.partial(kernel, slots, row_blocks, col_blocks, per, scale),
        out_shape=(
            jax.ShapeDtypeStruct((own, width), BF16),
            jax.ShapeDtypeStruct((width, width), F32),
            jax.ShapeDtypeStruct((own, width), BF16),
        ),
        in_specs=[anywhere] * 8,
        out_specs=(in_vmem,) * 3,
        scratch_shapes=[
            v((own, width), BF16),
            v((own, width), jnp.int32),
            v((width, width), BF16),
            v((own, width), BF16),
            v((1, slots), jnp.int32),
            v((1, slots), jnp.int32),
            pltpu.SMEM((1, 1), jnp.int32),
            v((8, PAD), jnp.int32),
            v((slots, tile, tile), BF16),
            v((8, PAD), jnp.int32),
            pltpu.SMEM((8, PAD), jnp.int32),
            v((col_blocks,) + block, BF16),
            v((row_blocks, width, tile), BF16),
            v((slots,) + block, BF16),
            v((row_blocks,) + block, BF16),
            v((col_blocks,) + block, BF16),
            v((2, 4, per) + block, BF16),
            v((2, 4, per) + block, BF16),
            v((2, 2, half) + block, BF16),
            v((2, 2, half) + block, BF16),
            v((2, 2, per) + block, BF16),
            v((2, 2, per) + block, BF16),
            v((2, per) + block, BF16),
            v((2, per) + block, BF16),
            v(block, F32),
            v((width, tile), F32),
            v((own, width), BF16),
            v((width, width), F32),
            v((width // 2, width), F32),
            v((4, width // 2, width), F32),
            v((4, width // 2, width), F32),
            v((4, width // 2, width), F32),
            v((2, width // 2, width), F32),
            pltpu.SemaphoreType.DMA((N_COPIES,)),
            pltpu.SemaphoreType.DMA((N_COPIES,)),
            pltpu.SemaphoreType.DMA((9,)),
        ],
        compiler_params=pltpu.CompilerParams(
            collective_id=0, has_side_effects=True, vmem_limit_bytes=67043328
        ),
        name="layer",
    )(features[0], relu_mask[0], weight, cotangent[0], tile_rows[0], tile_cols[0], tile_count, tiles[0, 0])
    return out_pre[None], weight_grad, input_grad[None]


def solution(mesh):
    placed = (
        P("col", "row", None),
        P("col", "row", None),
        P("row", "col", None, None, None),
        P("row", "col", None),
        P("row", "col", None),
        P("row", "col"),
        P(),
        P("row", "col", None),
    )
    return jax.shard_map(
        body,
        mesh=mesh,
        in_specs=placed,
        out_specs=(P("row", "col", None), P(), P("col", "row", None)),
        check_vma=False,
    )
```

```python
import functools

import jax
import jax.numpy as jnp
from jax import lax
from jax.experimental import pallas as pl
from jax.experimental.pallas import tpu as pltpu
from jax.sharding import PartitionSpec as P

MESH = pl.DeviceIdType.MESH
F32 = jnp.float32
BF16 = jnp.bfloat16
UNROLL = 46
N_COPIES = 128
PAD = 256


def sorted_slots(rows, cols, count, row_blocks, col_blocks):
    n = rows.shape[1]
    across = lax.broadcasted_iota(jnp.int32, (n, n), 1)
    downward = lax.broadcasted_iota(jnp.int32, (n, n), 0)
    ids = across[0:1]
    down_ids = downward[:, 0:1]
    dead = ids >= count

    def column(row):
        return jnp.sum(jnp.where(across == downward, row, 0), axis=1, keepdims=True)

    def one(target, source, targets, sources):
        key = jnp.where(dead, targets * sources + ids, target * sources + source)
        goal = jnp.where(dead, targets, target)
        goal_c = column(goal)
        before = key < column(key)
        rank = jnp.sum(jnp.where(before, 1, 0), axis=1, keepdims=True)
        again = jnp.sum(jnp.where(before & (goal == goal_c), 1, 0), axis=1, keepdims=True)
        head = jnp.where(again == 0, 1, 0)
        packed = down_ids * 256 + column(source) * 2 + head
        order = jnp.sum(jnp.where(rank == across, packed, 0), axis=0, keepdims=True)
        upto = jnp.sum(jnp.where(goal_c <= across, 1, 0), axis=0, keepdims=True)
        some = jnp.sum(jnp.where(goal_c == across, 1, 0), axis=0, keepdims=True)
        return order, jnp.maximum(upto - 1, 0) * 2 + jnp.where(some > 0, 1, 0)

    order_f, last_f = one(rows, cols, row_blocks, col_blocks)
    order_b, last_b = one(cols, rows, col_blocks, row_blocks)
    return order_f, order_b, last_f, last_b


def kernel(
    slots, row_blocks, col_blocks, per, scale,
    feat_hbm, mask_hbm, w_hbm, cot_hbm, rows_hbm, cols_hbm, count_hbm, tiles_hbm,
    out_ref, wg_ref, ig_ref,
    feat_v, mask_v, w_v, cot_v, rows_v, cols_v, count_s, pair_v, tiles_v, tab_v, tab,
    hid, grd, prods, fpart, bpart, sib, xsum,
    f_ra, f_rb, f_fr, f_fl, f_zs, f_zb, b_ra, b_rb, b_fr, b_fl, b_zs, b_zb,
    acc_f, acc_b, tb, ac, ax, ay, az, ws,
    send_sem, recv_sem, local_sem,
):
    r = lax.axis_index("row")
    c = lax.axis_index("col")
    zh, y = r // 4, lax.rem(r, 4)
    x, zl, core = c // 4, lax.rem(c // 2, 2), lax.rem(c, 2)

    def col_of(xx, zz, kk):
        return xx * 4 + zz * 2 + kk

    def at_x(step):
        return lax.rem(x + step, 4)

    def at_y(step):
        return lax.rem(y + step, 4)

    def x_dev(step):
        return {"row": r, "col": col_of(at_x(step), zl, core)}

    def y_dev(step):
        return {"row": zh * 4 + at_y(step), "col": c}

    sib_dev = {"row": r, "col": col_of(x, zl, 1 - core)}
    zl_dev = {"row": r, "col": col_of(x, 1 - zl, core)}
    zh_dev = {"row": (1 - zh) * 4 + y, "col": c}
    zz_dev = {"row": (1 - zh) * 4 + y, "col": col_of(x, 1 - zl, core)}
    right, left, up, down = x_dev(1), x_dev(3), y_dev(1), y_dev(3)
    peers = [sib_dev, right, left, x_dev(2), up, down, y_dev(2), zl_dev, zh_dev, zz_dev]

    barrier = pltpu.get_barrier_semaphore()
    for peer in peers:
        pl.semaphore_signal(barrier, inc=1, device_id=peer, device_id_type=MESH)

    loads = [
        (feat_hbm, feat_v), (mask_hbm, mask_v), (w_hbm, w_v), (cot_hbm, cot_v),
        (rows_hbm, rows_v), (cols_hbm, cols_v),
        (count_hbm, count_s), (tiles_hbm, tiles_v),
    ]
    loads = [pltpu.make_async_copy(src, dst, local_sem.at[i]) for i, (src, dst) in enumerate(loads)]
    for load in loads[:7]:
        load.start()

    made = []

    def send(src, dst, dev):
        i = len(made)
        copy = pltpu.make_async_remote_copy(
            src_ref=src, dst_ref=dst, send_sem=send_sem.at[i], recv_sem=recv_sem.at[i],
            device_id=dev, device_id_type=MESH,
        )
        copy.start()
        made.append(copy)
        return copy

    half = per // 2

    def col_shard(xx, zz, kk, first=0, size=per):
        return grd.at[pl.ds(col_of(xx, zz, kk) * per + first, size)]

    def row_shard(zz, yy, first=0, size=per):
        return hid.at[pl.ds((zz * 4 + yy) * per + first, size)]

    def share(ref, dev):
        return send(ref, ref, dev)

    first, second = (0, half), (half, half)

    loads[0].wait()
    loads[1].wait()
    loads[7].start()
    for j in range(per):
        rows = slice(j * 256, (j + 1) * 256)
        hid[r * per + j] = feat_v[rows] * mask_v[rows].astype(F32).astype(BF16)

    pl.semaphore_wait(barrier, len(peers))

    def spread_y(zz):
        a = share(row_shard(zz, y, *first), up)
        b = share(row_shard(zz, y, *second), down)
        return a, b, [share(row_shard(zz, y, *second), up), share(row_shard(zz, y, *first), down)]

    def relay_y(a, b, zz):
        a.wait_recv()
        on = [share(row_shard(zz, at_y(3), *first), up)]
        b.wait_recv()
        on.append(share(row_shard(zz, at_y(1), *second), down))
        return on

    def spread_x(zz):
        a = share(col_shard(x, zz, core, *first), right)
        b = share(col_shard(x, zz, core, *second), left)
        rest = [share(col_shard(x, zz, core, *second), right), share(col_shard(x, zz, core, *first), left)]
        c_s.append(share(col_shard(x, zz, core), sib_dev))
        return a, b, rest

    def relay_x(a, b, zz):
        a.wait_recv()
        on = [share(col_shard(at_x(3), zz, core, *first), right)]
        b.wait_recv()
        on.append(share(col_shard(at_x(1), zz, core, *second), left))
        return on

    def cross_near(rest, zz):
        rest[0].wait_recv()
        c_s.append(share(col_shard(at_x(3), zz, core), sib_dev))
        rest[1].wait_recv()
        c_s.append(share(col_shard(at_x(1), zz, core), sib_dev))

    def cross_far(on, zz):
        for copy in on:
            copy.wait_recv()
        c_s.append(share(col_shard(at_x(2), zz, core), sib_dev))

    def half_y(zz, ab):
        return share(row_shard(zz, y, *ab), up), share(row_shard(zz, y, *ab), down)

    def half_x(zz, ab):
        return share(col_shard(x, zz, core, *ab), right), share(col_shard(x, zz, core, *ab), left)

    def pass_y(copy, zz, ab, step, dev):
        copy.wait_recv()
        return share(row_shard(zz, at_y(step), *ab), dev)

    def pass_x(copy, zz, ab, step, dev):
        copy.wait_recv()
        return share(col_shard(at_x(step), zz, core, *ab), dev)

    c_s = []
    ra_y, rb_y, r_rest = spread_y(zh)
    r_za = share(row_shard(zh, y, *first), zh_dev)

    loads[2].wait()
    loads[3].wait()
    unit = lax.broadcasted_iota(jnp.int32, w_v.shape, 0) == lax.broadcasted_iota(jnp.int32, w_v.shape, 1)
    unit = jnp.where(unit, 1.0, 0.0).astype(BF16)
    for j in range(per):
        block = lax.dot_general(
            unit, cot_v[j * 256 : (j + 1) * 256], (((1,), (1,)), ((), ())), preferred_element_type=F32
        )
        grd[c * per + j] = block.astype(BF16)
    ca_x, cb_x, c_rest = spread_x(zl)
    c_za = share(col_shard(x, zl, core, *first), zl_dev)
    r_zb = share(row_shard(zh, y, *second), zh_dev)
    c_zb = share(col_shard(x, zl, core, *second), zl_dev)

    for load in loads[4:7]:
        load.wait()
    pair_v[...] = jnp.zeros_like(pair_v)
    pair_v[0:1, 0:slots] = rows_v[...]
    pair_v[1:2, 0:slots] = cols_v[...]
    table = sorted_slots(pair_v[0:1], pair_v[1:2], count_s[0, 0], row_blocks, col_blocks)
    for i, line in enumerate(table):
        tab_v[i : i + 1] = line
    to_smem = pltpu.make_async_copy(tab_v, tab, local_sem.at[8])
    to_smem.start()

    r_on = relay_y(ra_y, rb_y, zh)
    c_on = relay_x(ca_x, cb_x, zl)
    r_za.wait_recv()
    rza_u, rza_d = half_y(1 - zh, first)
    c_za.wait_recv()
    cza_r, cza_l = half_x(1 - zl, first)
    cross_near(c_rest, zl)
    r_zb.wait_recv()
    rzb_u, rzb_d = half_y(1 - zh, second)
    cross_far(c_on, zl)
    c_zb.wait_recv()
    czb_r, czb_l = half_x(1 - zl, second)
    c_s.append(share(col_shard(x, 1 - zl, core), sib_dev))
    rz_on = [pass_y(rza_u, 1 - zh, first, 3, up)]
    cz_on = [pass_x(cza_r, 1 - zl, first, 3, right)]
    rz_on.append(pass_y(rzb_d, 1 - zh, second, 1, down))
    cz_on.append(pass_x(czb_l, 1 - zl, second, 1, left))
    cz_rest = (czb_r, cza_l)
    to_smem.wait()
    loads[7].wait()
    for copy in (*r_rest, *r_on, rzb_u, rza_d, *rz_on):
        copy.wait_recv()

    low, high = slice(0, 128), slice(128, 256)
    parts = (low, high)

    def fwd_range(h, lo, hi):
        @pl.loop(lo, hi)
        def _(g):
            acc = acc_f[...]
            for u in range(UNROLL):
                p = g * UNROLL + u
                word = tab[0, p]
                prod = jnp.dot(tiles_v[word >> 8, parts[h], :], hid[(word >> 1) & 127], preferred_element_type=F32)
                acc = jnp.where((word & 1) == 1, 0.0, acc) + prod
                prods[p, parts[h], :] = acc.astype(BF16)
            acc_f[...] = acc

    def bwd_range(lo, hi):
        @pl.loop(lo, hi)
        def _(g):
            acc = acc_b[...]
            for u in range(UNROLL):
                p = g * UNROLL + u
                word = tab[1, p]
                prod = jnp.dot(grd[(word >> 1) & 127], tiles_v[word >> 8], preferred_element_type=F32)
                acc = jnp.where((word & 1) == 1, 0.0, acc) + prod
                prods[p, low, :] = acc[:, low].astype(BF16)
                prods[p, high, :] = acc[:, high].astype(BF16)
            acc_b[...] = acc

    groups = slots // UNROLL
    acc_f[...] = jnp.zeros_like(acc_f)
    acc_b[...] = jnp.zeros_like(acc_b)

    zs_of = (1 - zl, zl)
    sibs = {}

    def take_f(h, base):
        for j in range(per):
            word = tab[2, base + j]
            value = prods[word >> 1, parts[h], :]
            fpart[h, base + j] = jnp.where((word & 1) == 1, value, jnp.zeros_like(value))

    def fill_f(h):
        for dz in range(2):
            for dx in (2, 1, 3, 0):
                base = col_of(at_x(dx), zs_of[dz], 1 - core) * per
                take_f(h, base)
                sibs[h, dz, dx] = send(fpart.at[h, pl.ds(base, per)], sib.at[h, dz, dx], sib_dev)

        @pl.loop(0, row_blocks // (2 * per))
        def _(m):
            take_f(h, (2 * m + core) * per)

    def with_sibling(h, dz, dx):
        sibs[h, dz, dx].wait_recv()
        base = col_of(at_x(dx), zs_of[dz], core) * per
        for j in range(per):
            xsum[h, dz, dx, j] = (fpart[h, base + j].astype(F32) + sib[h, dz, dx, j].astype(F32)).astype(BF16)

    def add_into(dst, start, other):
        for j in range(half):
            dst[start + j] = (dst[start + j].astype(F32) + other[j].astype(F32)).astype(BF16)

    def ring_sum(ra, rb, fr, fl, zs, zb, part, prepare, ahead, behind, z_dev, finish):
        a, b = first, second

        def piece(dz, d, ab):
            return part(dz, d).at[pl.ds(ab[0], ab[1])]

        outer, inner = {}, {}

        def spread(dz):
            prepare(dz, 2)
            outer[dz] = (
                send(piece(dz, 2, a), ra.at[dz], ahead),
                send(piece(dz, 2, b), rb.at[dz], behind),
            )
            prepare(dz, 1)
            prepare(dz, 3)
            inner[dz] = [
                send(piece(dz, 1, b), fr.at[dz, pl.ds(half, half)], ahead),
                send(piece(dz, 3, a), fl.at[dz, pl.ds(0, half)], behind),
            ]

        def relay(dz):
            outer[dz][0].wait_recv()
            add_into(part(dz, 1), 0, ra.at[dz])
            inner[dz].append(send(piece(dz, 1, a), fr.at[dz, pl.ds(0, half)], ahead))
            outer[dz][1].wait_recv()
            add_into(part(dz, 3), half, rb.at[dz])
            inner[dz].append(send(piece(dz, 3, b), fl.at[dz, pl.ds(half, half)], behind))

        def total(dz, j):
            return part(dz, 0)[j].astype(F32) + fr[dz, j].astype(F32) + fl[dz, j].astype(F32)

        spread(0)
        yield
        relay(0)
        yield
        spread(1)
        prepare(0, 0)
        yield
        for copy in inner[0]:
            copy.wait_recv()
        for j in range(per):
            zs[j] = total(0, j).astype(BF16)
        last = send(zs, zb, z_dev)
        prepare(1, 0)
        yield
        relay(1)
        yield
        for copy in inner[1]:
            copy.wait_recv()
        last.wait_recv()
        for j in range(per):
            finish(j, total(1, j) + zb[j].astype(F32))

    def forward_sum(h):
        def finish(j, value):
            rows = slice(j * 256 + h * 128, j * 256 + h * 128 + 128)
            out_ref[rows] = jnp.dot(value.astype(BF16), w_v[...], preferred_element_type=F32).astype(BF16)

        return ring_sum(
            f_ra.at[h], f_rb.at[h], f_fr.at[h], f_fl.at[h], f_zs.at[h], f_zb.at[h],
            lambda dz, d: xsum.at[h, dz, d],
            functools.partial(with_sibling, h),
            right, left, zl_dev, finish,
        )

    def finish_b(j, value):
        for h in range(2):
            rows = slice(j * 256 + h * 128, j * 256 + h * 128 + 128)
            grad = lax.dot_general(
                value[parts[h]].astype(BF16), w_v[...], (((0,), (1,)), ((), ())), preferred_element_type=F32
            )
            ig_ref[rows] = (grad * mask_v[rows].astype(F32)).astype(BF16)

    zh_of = (1 - zh, zh)
    sum_b = ring_sum(
        b_ra, b_rb, b_fr, b_fl, b_zs, b_zb,
        lambda dz, d: bpart.at[pl.ds((zh_of[dz] * 4 + at_y(d)) * per, per)],
        lambda dz, d: None,
        up, down, zh_dev, finish_b,
    )

    def weight_sum():
        tb[...] = jnp.zeros_like(tb)

        @pl.loop(0, col_blocks // 16)
        def _(g):
            acc = tb[...]
            for u in range(16):
                i = g * 16 + u
                columns = jnp.concatenate([bpart[i, low, :], bpart[i, high, :]], axis=1)
                acc += jnp.dot(columns, hid[i], preferred_element_type=F32)
            tb[...] = acc

        rows = tb.shape[0] // 2
        to_sib = send(tb.at[pl.ds((1 - core) * rows, rows)], ac, sib_dev)
        yield
        to_sib.wait_recv()
        term = tb[pl.ds(core * rows, rows)] + ac[...]
        stages = (
            (az, zh * 2 + zl, [zl_dev, zh_dev, zz_dev]),
            (ax, x, [x_dev(step) for step in (1, 3, 2)]),
            (ay, y, [y_dev(step) for step in (1, 3, 2)]),
        )
        for held, at, devices in stages:
            held[at] = term
            copies = [send(held.at[at], held.at[at], dev) for dev in devices]
            yield
            for copy in copies:
                copy.wait_recv()
            term = (held[0] + held[1]) + (held[2] + held[3])
        ws[core] = term * scale
        last = share(ws.at[core], sib_dev)
        yield
        last.wait_recv()
        wg_ref[...] = jnp.concatenate([ws[0], ws[1]], axis=0).T

    f_lo, f_hi, wsum = forward_sum(0), forward_sum(1), weight_sum()

    fwd_range(0, 0, groups // 2)
    cross_near(cz_rest, 1 - zl)
    fwd_range(0, groups // 2, groups)
    fill_f(0)
    cross_far(cz_on, 1 - zl)
    for copy in c_s:
        copy.wait_recv()

    bwd_range(0, groups // 2)
    next(f_lo)
    bwd_range(groups // 2, groups)

    @pl.loop(0, col_blocks // per)
    def _(m):
        for j in range(per):
            word = tab[3, m * per + j]
            value = prods[word >> 1]
            bpart[m * per + j] = jnp.where((word & 1) == 1, value, jnp.zeros_like(value))

    next(sum_b)
    next(wsum)
    fwd_range(1, 0, groups // 4)
    next(f_lo)
    next(wsum)
    next(f_lo)
    fwd_range(1, groups // 4, groups // 2)
    next(wsum)
    fwd_range(1, groups // 2, groups)
    next(sum_b)
    fill_f(1)
    next(f_lo)
    next(f_lo)
    next(f_hi)
    next(sum_b)
    next(wsum)
    next(f_hi)
    next(f_hi)
    next(sum_b)
    next(f_lo, None)
    next(f_hi)
    next(sum_b)
    next(f_hi)
    next(wsum)
    next(f_hi, None)
    next(wsum, None)
    next(sum_b, None)

    for copy in made:
        copy.wait_send()


def keep(a_ref, b_ref, c_ref, a_out, b_out, c_out, sem):
    pairs = ((a_ref, a_out), (b_ref, b_out), (c_ref, c_out))
    copies = [pltpu.make_async_copy(src, dst, sem.at[i]) for i, (src, dst) in enumerate(pairs)]
    for copy in copies:
        copy.start()
    for copy in copies:
        copy.wait()


def body(features, relu_mask, tiles, tile_rows, tile_cols, tile_count, weight, cotangent):
    slots, tile = tiles.shape[2], tiles.shape[3]
    own, width = features.shape[1:]
    per = own // tile
    row_blocks, col_blocks = per * lax.axis_size("col"), per * lax.axis_size("row")
    half = per // 2
    scale = float((own * lax.axis_size("row") * lax.axis_size("col")) ** -0.5)
    block, small = (tile, width), (tile // 2, width)
    v = pltpu.VMEM

    def ring_buffers(lead, rows):
        shapes = [(2, half), (2, half), (2, per), (2, per), (per,), (per,)]
        return [v(lead + shape + rows, BF16) for shape in shapes]

    anywhere = pl.BlockSpec(memory_space=pl.ANY)
    in_vmem = pl.BlockSpec(memory_space=pltpu.VMEM)
    results = pl.pallas_call(
        functools.partial(kernel, slots, row_blocks, col_blocks, per, scale),
        out_shape=(
            jax.ShapeDtypeStruct((own, width), BF16),
            jax.ShapeDtypeStruct((width, width), F32),
            jax.ShapeDtypeStruct((own, width), BF16),
        ),
        in_specs=[anywhere] * 8,
        out_specs=(in_vmem,) * 3,
        scratch_shapes=[
            v((own, width), BF16),
            v((own, width), jnp.int32),
            v((width, width), BF16),
            v((own, width), BF16),
            v((1, slots), jnp.int32),
            v((1, slots), jnp.int32),
            pltpu.SMEM((1, 1), jnp.int32),
            v((8, PAD), jnp.int32),
            v((slots, tile, tile), BF16),
            v((8, PAD), jnp.int32),
            pltpu.SMEM((8, PAD), jnp.int32),
            v((col_blocks,) + block, BF16),
            v((row_blocks, width, tile), BF16),
            v((slots,) + block, BF16),
            v((2, row_blocks) + small, BF16),
            v((col_blocks,) + block, BF16),
            v((2, 2, 4, per) + small, BF16),
            v((2, 2, 4, per) + small, BF16),
            *ring_buffers((2,), small),
            *ring_buffers((), block),
            v(small, F32),
            v((width, tile), F32),
            v((width, width), F32),
            v((width // 2, width), F32),
            v((4, width // 2, width), F32),
            v((4, width // 2, width), F32),
            v((4, width // 2, width), F32),
            v((2, width // 2, width), F32),
            pltpu.SemaphoreType.DMA((N_COPIES,)),
            pltpu.SemaphoreType.DMA((N_COPIES,)),
            pltpu.SemaphoreType.DMA((9,)),
        ],
        compiler_params=pltpu.CompilerParams(
            collective_id=0, has_side_effects=True, vmem_limit_bytes=67043328
        ),
        name="layer",
    )(features[0], relu_mask[0], weight, cotangent[0], tile_rows[0], tile_cols[0], tile_count, tiles[0, 0])
    out_pre, weight_grad, input_grad = pl.pallas_call(
        keep,
        out_shape=[jax.ShapeDtypeStruct(value.shape, value.dtype) for value in results],
        in_specs=[in_vmem] * 3,
        out_specs=[anywhere] * 3,
        scratch_shapes=[pltpu.SemaphoreType.DMA((3,))],
        compiler_params=pltpu.CompilerParams(vmem_limit_bytes=4 * 1024 * 1024),
        name="keep",
    )(*results)
    return out_pre[None], weight_grad, input_grad[None]


def solution(mesh):
    placed = (
        P("col", "row", None),
        P("col", "row", None),
        P("row", "col", None, None, None),
        P("row", "col", None),
        P("row", "col", None),
        P("row", "col"),
        P(),
        P("row", "col", None),
    )
    return jax.shard_map(
        body,
        mesh=mesh,
        in_specs=placed,
        out_specs=(P("row", "col", None), P(), P("col", "row", None)),
        check_vma=False,
    )
```

```python
import functools

import jax
import jax.numpy as jnp
from jax import lax
from jax.experimental import pallas as pl
from jax.experimental.pallas import tpu as pltpu
from jax.sharding import PartitionSpec as P

MESH = pl.DeviceIdType.MESH
F32 = jnp.float32
BF16 = jnp.bfloat16
UNROLL = 46
N_COPIES = 128
PAD = 256


def sorted_slots(rows, cols, count, row_blocks, col_blocks):
    n = rows.shape[1]
    across = lax.broadcasted_iota(jnp.int32, (n, n), 1)
    downward = lax.broadcasted_iota(jnp.int32, (n, n), 0)
    ids = across[0:1]
    down_ids = downward[:, 0:1]
    dead = ids >= count

    def column(row):
        return jnp.sum(jnp.where(across == downward, row, 0), axis=1, keepdims=True)

    def one(target, source, targets, sources):
        key = jnp.where(dead, targets * sources + ids, target * sources + source)
        goal = jnp.where(dead, targets, target)
        goal_c = column(goal)
        before = key < column(key)
        rank = jnp.sum(jnp.where(before, 1, 0), axis=1, keepdims=True)
        again = jnp.sum(jnp.where(before & (goal == goal_c), 1, 0), axis=1, keepdims=True)
        head = jnp.where(again == 0, 1, 0)
        packed = down_ids * 256 + column(source) * 2 + head
        order = jnp.sum(jnp.where(rank == across, packed, 0), axis=0, keepdims=True)
        upto = jnp.sum(jnp.where(goal_c <= across, 1, 0), axis=0, keepdims=True)
        some = jnp.sum(jnp.where(goal_c == across, 1, 0), axis=0, keepdims=True)
        return order, jnp.maximum(upto - 1, 0) * 2 + jnp.where(some > 0, 1, 0)

    order_f, last_f = one(rows, cols, row_blocks, col_blocks)
    order_b, last_b = one(cols, rows, col_blocks, row_blocks)
    return order_f, order_b, last_f, last_b


def kernel(
    slots, row_blocks, col_blocks, per, scale,
    feat_hbm, mask_hbm, w_hbm, cot_hbm, rows_hbm, cols_hbm, count_hbm, tiles_hbm,
    out_ref, wg_ref, ig_ref,
    feat_v, mask_v, w_v, cot_v, rows_v, cols_v, count_s, pair_v, tiles_v, tab_v, tab,
    hid, grd, prods, fpart, bpart, sib, xsum,
    f_ra, f_rb, f_fr, f_fl, f_zs, f_zb, b_ra, b_rb, b_fr, b_fl, b_zs, b_zb,
    acc_f, acc_b, tb, ac, ax, ay, az, ws,
    send_sem, recv_sem, local_sem,
):
    r = lax.axis_index("row")
    c = lax.axis_index("col")
    zh, y = r // 4, lax.rem(r, 4)
    x, zl, core = c // 4, lax.rem(c // 2, 2), lax.rem(c, 2)

    def col_of(xx, zz, kk):
        return xx * 4 + zz * 2 + kk

    def at_x(step):
        return lax.rem(x + step, 4)

    def at_y(step):
        return lax.rem(y + step, 4)

    def x_dev(step):
        return {"row": r, "col": col_of(at_x(step), zl, core)}

    def y_dev(step):
        return {"row": zh * 4 + at_y(step), "col": c}

    sib_dev = {"row": r, "col": col_of(x, zl, 1 - core)}
    zl_dev = {"row": r, "col": col_of(x, 1 - zl, core)}
    zh_dev = {"row": (1 - zh) * 4 + y, "col": c}
    zz_dev = {"row": (1 - zh) * 4 + y, "col": col_of(x, 1 - zl, core)}
    right, left, up, down = x_dev(1), x_dev(3), y_dev(1), y_dev(3)
    peers = [sib_dev, right, left, x_dev(2), up, down, y_dev(2), zl_dev, zh_dev, zz_dev]

    barrier = pltpu.get_barrier_semaphore()
    for peer in peers:
        pl.semaphore_signal(barrier, inc=1, device_id=peer, device_id_type=MESH)

    loads = [
        (feat_hbm, feat_v), (mask_hbm, mask_v), (w_hbm, w_v), (cot_hbm, cot_v),
        (rows_hbm, rows_v), (cols_hbm, cols_v),
        (count_hbm, count_s), (tiles_hbm, tiles_v),
    ]
    loads = [pltpu.make_async_copy(src, dst, local_sem.at[i]) for i, (src, dst) in enumerate(loads)]
    for load in loads[:7]:
        load.start()

    made = []

    def send(src, dst, dev):
        i = len(made)
        copy = pltpu.make_async_remote_copy(
            src_ref=src, dst_ref=dst, send_sem=send_sem.at[i], recv_sem=recv_sem.at[i],
            device_id=dev, device_id_type=MESH,
        )
        copy.start()
        made.append(copy)
        return copy

    half = per // 2

    def col_shard(xx, zz, kk, first=0, size=per):
        return grd.at[pl.ds(col_of(xx, zz, kk) * per + first, size)]

    def row_shard(zz, yy, first=0, size=per):
        return hid.at[pl.ds((zz * 4 + yy) * per + first, size)]

    def share(ref, dev):
        return send(ref, ref, dev)

    first, second = (0, half), (half, half)

    loads[0].wait()
    loads[1].wait()
    loads[7].start()
    for j in range(per):
        rows = slice(j * 256, (j + 1) * 256)
        hid[r * per + j] = feat_v[rows] * mask_v[rows].astype(F32).astype(BF16)

    pl.semaphore_wait(barrier, len(peers))

    def spread_y(zz):
        a = share(row_shard(zz, y, *first), up)
        b = share(row_shard(zz, y, *second), down)
        return a, b, [share(row_shard(zz, y, *second), up), share(row_shard(zz, y, *first), down)]

    def relay_y(a, b, zz):
        a.wait_recv()
        on = [share(row_shard(zz, at_y(3), *first), up)]
        b.wait_recv()
        on.append(share(row_shard(zz, at_y(1), *second), down))
        return on

    def spread_x(zz):
        a = share(col_shard(x, zz, core, *first), right)
        b = share(col_shard(x, zz, core, *second), left)
        rest = [share(col_shard(x, zz, core, *second), right), share(col_shard(x, zz, core, *first), left)]
        c_s.append(share(col_shard(x, zz, core), sib_dev))
        return a, b, rest

    def relay_x(a, b, zz):
        a.wait_recv()
        on = [share(col_shard(at_x(3), zz, core, *first), right)]
        b.wait_recv()
        on.append(share(col_shard(at_x(1), zz, core, *second), left))
        return on

    def cross_near(rest, zz):
        rest[0].wait_recv()
        c_s.append(share(col_shard(at_x(3), zz, core), sib_dev))
        rest[1].wait_recv()
        c_s.append(share(col_shard(at_x(1), zz, core), sib_dev))

    def cross_far(on, zz):
        for copy in on:
            copy.wait_recv()
        c_s.append(share(col_shard(at_x(2), zz, core), sib_dev))

    def half_y(zz, ab):
        return share(row_shard(zz, y, *ab), up), share(row_shard(zz, y, *ab), down)

    def half_x(zz, ab):
        return share(col_shard(x, zz, core, *ab), right), share(col_shard(x, zz, core, *ab), left)

    def pass_y(copy, zz, ab, step, dev):
        copy.wait_recv()
        return share(row_shard(zz, at_y(step), *ab), dev)

    def pass_x(copy, zz, ab, step, dev):
        copy.wait_recv()
        return share(col_shard(at_x(step), zz, core, *ab), dev)

    c_s = []
    ra_y, rb_y, r_rest = spread_y(zh)
    r_za = share(row_shard(zh, y, *first), zh_dev)

    loads[2].wait()
    loads[3].wait()
    unit = lax.broadcasted_iota(jnp.int32, w_v.shape, 0) == lax.broadcasted_iota(jnp.int32, w_v.shape, 1)
    unit = jnp.where(unit, 1.0, 0.0).astype(BF16)
    for j in range(per):
        block = lax.dot_general(
            unit, cot_v[j * 256 : (j + 1) * 256], (((1,), (1,)), ((), ())), preferred_element_type=F32
        )
        grd[c * per + j] = block.astype(BF16)
    ca_x, cb_x, c_rest = spread_x(zl)
    c_za = share(col_shard(x, zl, core, *first), zl_dev)
    r_zb = share(row_shard(zh, y, *second), zh_dev)
    c_zb = share(col_shard(x, zl, core, *second), zl_dev)

    for load in loads[4:7]:
        load.wait()
    pair_v[...] = jnp.zeros_like(pair_v)
    pair_v[0:1, 0:slots] = rows_v[...]
    pair_v[1:2, 0:slots] = cols_v[...]
    table = sorted_slots(pair_v[0:1], pair_v[1:2], count_s[0, 0], row_blocks, col_blocks)
    for i, line in enumerate(table):
        tab_v[i : i + 1] = line
    to_smem = pltpu.make_async_copy(tab_v, tab, local_sem.at[8])
    to_smem.start()

    r_on = relay_y(ra_y, rb_y, zh)
    c_on = relay_x(ca_x, cb_x, zl)
    r_za.wait_recv()
    rza_u, rza_d = half_y(1 - zh, first)
    c_za.wait_recv()
    cza_r, cza_l = half_x(1 - zl, first)
    cross_near(c_rest, zl)
    r_zb.wait_recv()
    rzb_u, rzb_d = half_y(1 - zh, second)
    cross_far(c_on, zl)
    c_zb.wait_recv()
    czb_r, czb_l = half_x(1 - zl, second)
    c_s.append(share(col_shard(x, 1 - zl, core), sib_dev))
    rz_on = [pass_y(rza_u, 1 - zh, first, 3, up)]
    cz_on = [pass_x(cza_r, 1 - zl, first, 3, right)]
    rz_on.append(pass_y(rzb_d, 1 - zh, second, 1, down))
    cz_on.append(pass_x(czb_l, 1 - zl, second, 1, left))
    cz_rest = (czb_r, cza_l)
    to_smem.wait()
    loads[7].wait()
    for copy in (*r_rest, *r_on, rzb_u, rza_d, *rz_on):
        copy.wait_recv()

    low, high = slice(0, 128), slice(128, 256)
    parts = (low, high)

    def fwd_range(h, lo, hi):
        @pl.loop(lo, hi)
        def _(g):
            acc = acc_f[...]
            for u in range(UNROLL):
                p = g * UNROLL + u
                word = tab[0, p]
                prod = jnp.dot(tiles_v[word >> 8, parts[h], :], hid[(word >> 1) & 127], preferred_element_type=F32)
                acc = jnp.where((word & 1) == 1, 0.0, acc) + prod
                prods[p, parts[h], :] = acc.astype(BF16)
            acc_f[...] = acc

    def bwd_range(lo, hi):
        @pl.loop(lo, hi)
        def _(g):
            acc = acc_b[...]
            for u in range(UNROLL):
                p = g * UNROLL + u
                word = tab[1, p]
                prod = jnp.dot(grd[(word >> 1) & 127], tiles_v[word >> 8], preferred_element_type=F32)
                acc = jnp.where((word & 1) == 1, 0.0, acc) + prod
                prods[p, low, :] = acc[:, low].astype(BF16)
                prods[p, high, :] = acc[:, high].astype(BF16)
            acc_b[...] = acc

    groups = slots // UNROLL
    acc_f[...] = jnp.zeros_like(acc_f)
    acc_b[...] = jnp.zeros_like(acc_b)

    zs_of = (1 - zl, zl)
    sibs = {}

    def take_f(h, base):
        for j in range(per):
            word = tab[2, base + j]
            value = prods[word >> 1, parts[h], :]
            fpart[h, base + j] = jnp.where((word & 1) == 1, value, jnp.zeros_like(value))

    def fill_f(h):
        for dz in range(2):
            for dx in (2, 1, 3, 0):
                base = col_of(at_x(dx), zs_of[dz], 1 - core) * per
                take_f(h, base)
                sibs[h, dz, dx] = send(fpart.at[h, pl.ds(base, per)], sib.at[h, dz, dx], sib_dev)

        @pl.loop(0, row_blocks // (2 * per))
        def _(m):
            take_f(h, (2 * m + core) * per)

    def with_sibling(h, dz, dx):
        sibs[h, dz, dx].wait_recv()
        base = col_of(at_x(dx), zs_of[dz], core) * per
        for j in range(per):
            xsum[h, dz, dx, j] = (fpart[h, base + j].astype(F32) + sib[h, dz, dx, j].astype(F32)).astype(BF16)

    def add_into(dst, start, other):
        for j in range(half):
            dst[start + j] = (dst[start + j].astype(F32) + other[j].astype(F32)).astype(BF16)

    def ring_sum(ra, rb, fr, fl, zs, zb, part, prepare, ahead, behind, z_dev, finish):
        a, b = first, second

        def piece(dz, d, ab):
            return part(dz, d).at[pl.ds(ab[0], ab[1])]

        outer, inner = {}, {}

        def spread(dz):
            prepare(dz, 2)
            outer[dz] = (
                send(piece(dz, 2, a), ra.at[dz], ahead),
                send(piece(dz, 2, b), rb.at[dz], behind),
            )
            prepare(dz, 1)
            prepare(dz, 3)
            inner[dz] = [
                send(piece(dz, 1, b), fr.at[dz, pl.ds(half, half)], ahead),
                send(piece(dz, 3, a), fl.at[dz, pl.ds(0, half)], behind),
            ]

        def relay(dz):
            outer[dz][0].wait_recv()
            add_into(part(dz, 1), 0, ra.at[dz])
            inner[dz].append(send(piece(dz, 1, a), fr.at[dz, pl.ds(0, half)], ahead))
            outer[dz][1].wait_recv()
            add_into(part(dz, 3), half, rb.at[dz])
            inner[dz].append(send(piece(dz, 3, b), fl.at[dz, pl.ds(half, half)], behind))

        def total(dz, j):
            return part(dz, 0)[j].astype(F32) + fr[dz, j].astype(F32) + fl[dz, j].astype(F32)

        spread(0)
        yield
        relay(0)
        yield
        spread(1)
        prepare(0, 0)
        yield
        for copy in inner[0]:
            copy.wait_recv()
        for j in range(per):
            zs[j] = total(0, j).astype(BF16)
        last = send(zs, zb, z_dev)
        prepare(1, 0)
        yield
        relay(1)
        yield
        for copy in inner[1]:
            copy.wait_recv()
        last.wait_recv()
        for j in range(per):
            finish(j, total(1, j) + zb[j].astype(F32))

    def forward_sum(h):
        def finish(j, value):
            rows = slice(j * 256 + h * 128, j * 256 + h * 128 + 128)
            out_ref[rows] = jnp.dot(value.astype(BF16), w_v[...], preferred_element_type=F32).astype(BF16)

        return ring_sum(
            f_ra.at[h], f_rb.at[h], f_fr.at[h], f_fl.at[h], f_zs.at[h], f_zb.at[h],
            lambda dz, d: xsum.at[h, dz, d],
            functools.partial(with_sibling, h),
            right, left, zl_dev, finish,
        )

    def finish_b(j, value):
        for h in range(2):
            rows = slice(j * 256 + h * 128, j * 256 + h * 128 + 128)
            grad = lax.dot_general(
                value[parts[h]].astype(BF16), w_v[...], (((0,), (1,)), ((), ())), preferred_element_type=F32
            )
            ig_ref[rows] = (grad * mask_v[rows].astype(F32)).astype(BF16)

    zh_of = (1 - zh, zh)
    sum_b = ring_sum(
        b_ra, b_rb, b_fr, b_fl, b_zs, b_zb,
        lambda dz, d: bpart.at[pl.ds((zh_of[dz] * 4 + at_y(d)) * per, per)],
        lambda dz, d: None,
        up, down, zh_dev, finish_b,
    )

    def weight_sum():
        tb[...] = jnp.zeros_like(tb)

        @pl.loop(0, col_blocks // 16)
        def _(g):
            acc = tb[...]
            for u in range(16):
                i = g * 16 + u
                columns = jnp.concatenate([bpart[i, low, :], bpart[i, high, :]], axis=1)
                acc += jnp.dot(columns, hid[i], preferred_element_type=F32)
            tb[...] = acc

        rows = tb.shape[0] // 2
        to_sib = send(tb.at[pl.ds((1 - core) * rows, rows)], ac, sib_dev)
        yield
        to_sib.wait_recv()
        term = tb[pl.ds(core * rows, rows)] + ac[...]
        stages = (
            (az, zh * 2 + zl, [zl_dev, zh_dev, zz_dev]),
            (ax, x, [x_dev(step) for step in (1, 3, 2)]),
            (ay, y, [y_dev(step) for step in (1, 3, 2)]),
        )
        for held, at, devices in stages:
            held[at] = term
            copies = [send(held.at[at], held.at[at], dev) for dev in devices]
            yield
            for copy in copies:
                copy.wait_recv()
            term = (held[0] + held[1]) + (held[2] + held[3])
        ws[core] = term * scale
        last = share(ws.at[core], sib_dev)
        yield
        last.wait_recv()
        wg_ref[...] = jnp.concatenate([ws[0], ws[1]], axis=0).T

    f_lo, f_hi, wsum = forward_sum(0), forward_sum(1), weight_sum()

    fwd_range(0, 0, groups // 2)
    cross_near(cz_rest, 1 - zl)
    fwd_range(0, groups // 2, groups)
    fill_f(0)
    cross_far(cz_on, 1 - zl)
    for copy in c_s:
        copy.wait_recv()

    bwd_range(0, groups // 2)
    next(f_lo)
    bwd_range(groups // 2, groups)

    @pl.loop(0, col_blocks // per)
    def _(m):
        for j in range(per):
            word = tab[3, m * per + j]
            value = prods[word >> 1]
            bpart[m * per + j] = jnp.where((word & 1) == 1, value, jnp.zeros_like(value))

    next(sum_b)
    next(wsum)
    fwd_range(1, 0, groups // 4)
    next(f_lo)
    next(wsum)
    next(f_lo)
    fwd_range(1, groups // 4, groups // 2)
    next(wsum)
    fwd_range(1, groups // 2, groups)
    next(sum_b)
    fill_f(1)
    next(f_lo)
    next(f_lo)
    next(f_hi)
    next(sum_b)
    next(wsum)
    next(f_hi)
    next(f_hi)
    next(sum_b)
    next(f_lo, None)
    next(f_hi)
    next(sum_b)
    next(f_hi)
    next(wsum)
    next(f_hi, None)
    next(wsum, None)
    next(sum_b, None)

    for copy in made:
        copy.wait_send()


def keep(a_ref, b_ref, c_ref, a_out, b_out, c_out, a_v, b_v, c_v, sem):
    triples = ((a_ref, a_v, a_out), (b_ref, b_v, b_out), (c_ref, c_v, c_out))
    reads = [pltpu.make_async_copy(src, held, sem.at[i]) for i, (src, held, _) in enumerate(triples)]
    writes = [pltpu.make_async_copy(held, dst, sem.at[3 + i]) for i, (_, held, dst) in enumerate(triples)]
    for read in reads:
        read.start()
    for read, write in zip(reads, writes):
        read.wait()
        write.start()
    for write in writes:
        write.wait()


def body(features, relu_mask, tiles, tile_rows, tile_cols, tile_count, weight, cotangent):
    slots, tile = tiles.shape[2], tiles.shape[3]
    own, width = features.shape[1:]
    per = own // tile
    row_blocks, col_blocks = per * lax.axis_size("col"), per * lax.axis_size("row")
    half = per // 2
    scale = float((own * lax.axis_size("row") * lax.axis_size("col")) ** -0.5)
    block, small = (tile, width), (tile // 2, width)
    v = pltpu.VMEM

    def ring_buffers(lead, rows):
        shapes = [(2, half), (2, half), (2, per), (2, per), (per,), (per,)]
        return [v(lead + shape + rows, BF16) for shape in shapes]

    anywhere = pl.BlockSpec(memory_space=pl.ANY)
    in_vmem = pl.BlockSpec(memory_space=pltpu.VMEM)
    results = pl.pallas_call(
        functools.partial(kernel, slots, row_blocks, col_blocks, per, scale),
        out_shape=(
            jax.ShapeDtypeStruct((own, width), BF16),
            jax.ShapeDtypeStruct((width, width), F32),
            jax.ShapeDtypeStruct((own, width), BF16),
        ),
        in_specs=[anywhere] * 8,
        out_specs=(in_vmem,) * 3,
        scratch_shapes=[
            v((own, width), BF16),
            v((own, width), jnp.int32),
            v((width, width), BF16),
            v((own, width), BF16),
            v((1, slots), jnp.int32),
            v((1, slots), jnp.int32),
            pltpu.SMEM((1, 1), jnp.int32),
            v((8, PAD), jnp.int32),
            v((slots, tile, tile), BF16),
            v((8, PAD), jnp.int32),
            pltpu.SMEM((8, PAD), jnp.int32),
            v((col_blocks,) + block, BF16),
            v((row_blocks, width, tile), BF16),
            v((slots,) + block, BF16),
            v((2, row_blocks) + small, BF16),
            v((col_blocks,) + block, BF16),
            v((2, 2, 4, per) + small, BF16),
            v((2, 2, 4, per) + small, BF16),
            *ring_buffers((2,), small),
            *ring_buffers((), block),
            v(small, F32),
            v((width, tile), F32),
            v((width, width), F32),
            v((width // 2, width), F32),
            v((4, width // 2, width), F32),
            v((4, width // 2, width), F32),
            v((4, width // 2, width), F32),
            v((2, width // 2, width), F32),
            pltpu.SemaphoreType.DMA((N_COPIES,)),
            pltpu.SemaphoreType.DMA((N_COPIES,)),
            pltpu.SemaphoreType.DMA((9,)),
        ],
        compiler_params=pltpu.CompilerParams(
            collective_id=0, has_side_effects=True, vmem_limit_bytes=67043328
        ),
        name="layer",
    )(features[0], relu_mask[0], weight, cotangent[0], tile_rows[0], tile_cols[0], tile_count, tiles[0, 0])
    out_pre, weight_grad, input_grad = pl.pallas_call(
        keep,
        out_shape=[jax.ShapeDtypeStruct(value.shape, value.dtype) for value in results],
        in_specs=[anywhere] * 3,
        out_specs=[anywhere] * 3,
        scratch_shapes=[v(value.shape, value.dtype) for value in results] + [pltpu.SemaphoreType.DMA((6,))],
        compiler_params=pltpu.CompilerParams(vmem_limit_bytes=67043328),
        name="keep",
    )(*results)
    return out_pre[None], weight_grad, input_grad[None]


def solution(mesh):
    placed = (
        P("col", "row", None),
        P("col", "row", None),
        P("row", "col", None, None, None),
        P("row", "col", None),
        P("row", "col", None),
        P("row", "col"),
        P(),
        P("row", "col", None),
    )
    return jax.shard_map(
        body,
        mesh=mesh,
        in_specs=placed,
        out_specs=(P("row", "col", None), P(), P("col", "row", None)),
        check_vma=False,
    )
```
